32 devices in a mesh: group: 4 (over y, x), shard: 8 (over z, core).
Axes of the slice: x: 2, y: 2, z: 4, core: 2. Of those that a mesh axis runs over, the one named last changes fastest.
Arguments:
- queries: bfloat16 [32, 32, 128], P(('group', 'shard')), may hold values from -0.625 to 0.625
- passages: bfloat16 [4096, 128, 128], P(('group', 'shard')), may hold values from -0.5 to 0.5
- lengths: int32 [4096], P(('group', 'shard')), may hold values from 1 to 128
- cand_owner: int32 [32, 1024, 1], P(('group', 'shard')), may hold values from 0 to 31; in each aligned block of 1024 rows (0 to 1023, 1024 to 2047, ..., all dimensions but the last counted through in order) at most 48 rows name the same one
- cand_slot: int32 [32, 1024], P(('group', 'shard')), may hold values from 0 to 127
Outputs:
- scores: float32 [32, 1024], P(('group', 'shard'))
- best_scores: float32 [32, 100], P(('group', 'shard'))
The draws below stay inside these ranges and needn't reach their ends.
Inputs may be any that keep to these rules, and one draw needn't show every extreme that they name: `cand_owner`: the 1024 candidate rows of one device name any one owner at most 48 times, and some device names some owner exactly 48 times.
All inputs are finite; a program needn't handle non-finite values.
Results may differ from the reference program's by a relative error of at most 0.0003.
Values may be sent and summed in bfloat16 or wider, within the bound.
No kernel may reach another device: no remote copies, remote signals or barrier semaphores. Data moves between devices by JAX's collectives and lax.ppermute only.
A program may use at most 128 MiB of HBM per device.

```python
import math
import jax
import jax.numpy as jnp
import numpy as np
from jax import lax

DIM = 128
QT = 32
PT = 128
CAND = 1024
TOPK = 100
Q_DEV = 1
P_DEV = 128
Q = 32
PASSAGES = 4096
ROUTE_CAP = 48
DEVICES = 32


def set_ends(values, rng, smallest, high):
    index_at = [jax.random.randint(jax.random.fold_in(rng, axis), (), 0, length) for axis, length in enumerate(values.shape)]
    main_axis = values.shape.index(max(values.shape))
    neighbour = index_at[:main_axis] + [(index_at[main_axis] + 1) % values.shape[main_axis]] + index_at[main_axis + 1:]
    return values.at[tuple(index_at)].set(smallest).at[tuple(neighbour)].set(high)


def levels(own_key, shape, pieces, least, top_value):
    factor_of = 1.0
    for dim, parts in pieces:
        heights = jax.random.uniform(jax.random.fold_in(jax.random.fold_in(own_key, 6), dim), (parts,), jnp.float32, least / len(pieces), top_value / len(pieces))
        factor_of = factor_of * jnp.repeat(jnp.exp(heights), shape[dim] // parts).reshape((-1,) + (1,) * (len(shape) - 1 - dim))
    return factor_of


def routed_block(key, own, number, rows, amount, top, bound, skew):
    order = jax.random.permutation(key, amount)
    heavy_load, common = shares(amount, rows * top, bound, skew, True), shares(amount, rows * top, bound, skew, False)
    places = jnp.arange(amount)

    def named(sizes, rotation):
        used = int((sizes > 0).sum())
        fixed = max(1, used // 4)
        passed = fixed + (places - fixed + rotation * (used - fixed)) % max(1, amount - fixed)
        return jnp.zeros((amount,), jnp.int32).at[order[jnp.where(places < fixed, places, passed)]].set(jnp.asarray(sizes, jnp.int32))

    sizes = jnp.where(number % 4 == 0, named(heavy_load, number // 4), named(common, number - number // 4 - 1))
    mixed = jax.random.permutation(jax.random.fold_in(own, 3), amount)
    source_of, taker = mixed[0:amount // 2 * 2:2], mixed[1:amount // 2 * 2:2]
    slack = jnp.minimum(sizes[source_of] - 1, bound - sizes[taker]) // 2
    slack = jnp.where((source_of == order[0]) | (taker == order[0]) | (sizes[taker] == 0), 0, jnp.maximum(slack, 0))
    passed = jax.random.randint(jax.random.fold_in(own, 4), (amount // 2,), 0, 1 << 20) % (slack + 1)
    sizes = sizes.at[source_of].add(-passed).at[taker].add(passed)
    labels = jnp.searchsorted(jnp.cumsum(sizes), jnp.arange(rows * top), side="right").astype(jnp.int32)
    grid = labels.reshape(top, rows).T
    grid = grid[jax.random.permutation(jax.random.fold_in(own, 1), rows)]
    rotation = jax.random.randint(jax.random.fold_in(own, 2), (rows, 1), 0, top)
    return jnp.take_along_axis(grid, (jnp.arange(top)[None, :] + rotation) % top, axis=1)


def shares(number_of, total, reach, slope, full):
    weights = [(1 << 20) // math.isqrt(grade ** slope) + 1 for grade in range(1, number_of + 1)]
    largest = reach if full else min(reach, max(-(-total // number_of), total * weights[0] // sum(weights)))
    least = 1 if total - largest >= number_of - 1 else 0
    holding, rest = [largest] + [least] * (number_of - 1), total - largest - least * (number_of - 1)
    while rest > 0:
        free = [i for i in range(1, number_of) if holding[i] < largest] or [i for i in range(1, number_of) if holding[i] < reach]
        mass, budget = sum([weights[i] for i in free]), rest
        for i in free:
            more = min(reach - holding[i], max(1, budget * weights[i] // mass), rest)
            holding[i] = holding[i] + more
            rest = rest - more
    return np.array(holding)


def gaussian(key, extent, spread, most, split=(), kind=jnp.bfloat16):
    values = spread * jax.random.normal(key, extent, jnp.float32)
    if split:
        values = values * levels(key, extent, split, -0.22, 0.18)
    return jnp.clip(values, -most, most).astype(kind)


def setup_inputs(seed: int = 0) -> dict:
    key_of = jax.random.split(jax.random.key(seed), 6)
    queries = gaussian(key_of[0], (Q, QT, DIM), 0.1, 0.625, ((0, 32),))
    passages = gaussian(key_of[1], (PASSAGES, PT, DIM), DIM ** -0.5, 0.5, ((0, 32),))
    lengths = set_ends(jax.random.randint(key_of[2], (PASSAGES,), 1, PT + 1), jax.random.fold_in(key_of[2], 1), 1, PT).astype(jnp.int32)
    cand_owner_keys = jax.random.split(jax.random.fold_in(key_of[3], 1), Q * CAND // (Q_DEV * CAND))
    cand_owner_turns = jax.random.permutation(jax.random.fold_in(key_of[3], 3), Q * CAND // (Q_DEV * CAND))
    cand_owner = jax.vmap(lambda own, number: routed_block(jax.random.fold_in(key_of[3], 2), own, number, Q_DEV * CAND, DEVICES, 1, ROUTE_CAP, 2))(cand_owner_keys, cand_owner_turns).reshape((Q, CAND, 1))
    cand_slot = set_ends(jax.random.randint(key_of[4], (Q, CAND), 0, P_DEV), jax.random.fold_in(key_of[4], 1), 0, P_DEV - 1).astype(jnp.int32)
    return {"queries": queries, "passages": passages, "lengths": lengths, "cand_owner": cand_owner, "cand_slot": cand_slot}


NEGATIVE = -1.0e30


def reference(queries, passages, lengths, cand_owner, cand_slot):
    passage_ids = (cand_owner[:, :, 0] * P_DEV + cand_slot).astype(jnp.int32)
    token_places = jnp.arange(PT, dtype=jnp.int32)

    def one_query(packed):
        query_tokens, id_row = packed
        passage_tiles = passages[id_row].astype(jnp.float32)
        similarity = jnp.einsum("qd,ctd->cqt", query_tokens.astype(jnp.float32), passage_tiles)
        limits = lengths[id_row]
        similarity = jnp.where(token_places[None, None, :] < limits[:, None, None], similarity, NEGATIVE)
        return jnp.sum(jnp.max(similarity, axis=2), axis=1)

    scores = lax.map(one_query, (queries, passage_ids))
    best_scores = lax.top_k(scores, TOPK)[0]
    return scores, best_scores
```

```python
import jax
import jax.numpy as jnp
from jax import lax
from jax.experimental import pallas as pl
from jax.experimental.pallas import tpu as pltpu
from jax.sharding import PartitionSpec as P

TOPK = 100
NEGATIVE = -1e30
LANES = 128
AXES = ("group", "shard")


def score_body(lengths_ref, passages_ref, queries_ref, scores_ref, transposed_ref, best_ref):
    step = pl.program_id(1)
    query_count, query_tokens, depth = queries_ref.shape
    block, passage_tokens, _ = passages_ref.shape
    columns = query_count * query_tokens

    @pl.when(step == 0)
    def _():
        transposed_ref[...] = queries_ref[...].reshape(columns, depth).T

    rows = passages_ref[...].reshape(block * passage_tokens, depth)
    width = min(256, columns)
    for start in range(0, columns, width):
        similarity = jnp.dot(
            rows, transposed_ref[:, start : start + width], preferred_element_type=jnp.float32
        ).reshape(block, passage_tokens, width)
        token = lax.broadcasted_iota(jnp.int32, (passage_tokens, width), 0)
        for j in range(block):
            limited = jnp.where(token < lengths_ref[step * block + j], similarity[j], NEGATIVE)
            best_ref[pl.ds(step * block + j, 1), start : start + width] = jnp.max(
                limited, axis=0, keepdims=True
            )

    @pl.when(step == pl.num_programs(1) - 1)
    def _():
        query = lax.broadcasted_iota(jnp.int32, (query_count, columns), 0)
        column = lax.broadcasted_iota(jnp.int32, (query_count, columns), 1)
        first = query * query_tokens
        mine = ((column >= first) & (column < first + query_tokens)).astype(jnp.float32)
        scores_ref[...] = lax.dot_general(
            mine,
            best_ref[...],
            (((1,), (1,)), ((), ())),
            precision=lax.Precision.HIGHEST,
            preferred_element_type=jnp.float32,
        )


def score_all(queries, passages, lengths):
    query_total, query_tokens, depth = queries.shape
    passage_total, passage_tokens, _ = passages.shape
    tile = min(query_total, 32)
    block = min(passage_total, 16)
    columns = tile * query_tokens
    return pl.pallas_call(
        score_body,
        out_shape=jax.ShapeDtypeStruct((query_total, passage_total), jnp.float32),
        grid_spec=pltpu.PrefetchScalarGridSpec(
            num_scalar_prefetch=1,
            grid=(query_total // tile, passage_total // block),
            in_specs=[
                pl.BlockSpec((block, passage_tokens, depth), lambda q, i, _: (i, 0, 0)),
                pl.BlockSpec((tile, query_tokens, depth), lambda q, i, _: (q, 0, 0)),
            ],
            out_specs=pl.BlockSpec((tile, passage_total), lambda q, i, _: (q, 0)),
            scratch_shapes=[
                pltpu.VMEM((depth, columns), jnp.bfloat16),
                pltpu.VMEM((passage_total, columns), jnp.float32),
            ],
        ),
        name="maxsim",
    )(lengths, passages, queries)


def pick_body(table_ref, owner_ref, slot_ref, scores_ref, best_ref):
    owners, passages = table_ref.shape
    chunks = owner_ref.shape[1] // LANES

    def grid_of(ref):
        return jnp.concatenate(
            [ref[:, r * LANES : (r + 1) * LANES] for r in range(chunks)], axis=0
        )

    owner = grid_of(owner_ref)
    slot = grid_of(slot_ref)
    picked = jnp.zeros(owner.shape, jnp.float32)
    for o in range(owners):
        row = jnp.broadcast_to(table_ref[o : o + 1, :], owner.shape[:1] + (passages,))
        picked = jnp.where(owner == o, jnp.take_along_axis(row, slot, axis=1), picked)
    for r in range(chunks):
        scores_ref[:, r * LANES : (r + 1) * LANES] = picked[r : r + 1]

    square = (LANES, LANES)
    lower = lax.broadcasted_iota(jnp.int32, square, 0) < lax.broadcasted_iota(jnp.int32, square, 1)
    along = [jnp.broadcast_to(picked[r : r + 1], square) for r in range(chunks)]
    down = [a.T for a in along]
    place = lax.broadcasted_iota(jnp.int32, square, 0)
    kept = jnp.zeros(square, jnp.float32)
    for i in range(chunks):
        ahead = jnp.zeros(square, jnp.int32)
        for j in range(chunks):
            if j < i:
                wins = down[j] >= along[i]
            elif j > i:
                wins = down[j] > along[i]
            else:
                wins = (down[j] > along[i]) | ((down[j] == along[i]) & lower)
            ahead = ahead + wins.astype(jnp.int32)
        rank = jnp.sum(ahead, axis=0, keepdims=True)
        kept = kept + jnp.where(place == rank, along[i], 0.0)
    best_ref[...] = jnp.sum(kept.T, axis=0, keepdims=True)[:, : best_ref.shape[1]]


def pick(table, owner, slot):
    rows, candidates = slot.shape
    return pl.pallas_call(
        pick_body,
        out_shape=(
            jax.ShapeDtypeStruct((rows, candidates), jnp.float32),
            jax.ShapeDtypeStruct((rows, TOPK), jnp.float32),
        ),
        name="pick",
    )(table, owner, slot)


def shards(queries, passages, lengths, cand_owner, cand_slot):
    device_total = lax.axis_size("group") * lax.axis_size("shard")
    query_local, candidates = cand_slot.shape
    sent = jnp.broadcast_to(queries, (device_total,) + queries.shape[1:])
    everyone = lax.all_to_all(sent, AXES, split_axis=0, concat_axis=0, tiled=True)
    scores = score_all(everyone, passages, lengths)
    table = lax.all_to_all(scores, AXES, split_axis=0, concat_axis=0, tiled=True)
    return pick(table, cand_owner.reshape(query_local, candidates), cand_slot)


def solution(mesh):
    placed = (
        P(AXES, None, None),
        P(AXES, None, None),
        P(AXES),
        P(AXES, None, None),
        P(AXES, None),
    )
    return jax.shard_map(
        shards,
        mesh=mesh,
        in_specs=placed,
        out_specs=(P(AXES, None), P(AXES, None)),
        check_vma=False,
    )
```

```python
import functools

import jax
import jax.numpy as jnp
from jax import lax
from jax.experimental import pallas as pl
from jax.experimental.pallas import tpu as pltpu
from jax.sharding import PartitionSpec as P

TOPK = 100
NEGATIVE = -1e30
LANES = 128
SUBLANES = 8
PITCH = SUBLANES + 1
CHUNK = 16
BLOCK = 64
KERNEL_VMEM = 24 << 20
AXES = ("group", "shard")
WHOLE = pl.BlockSpec(memory_space=pltpu.VMEM)
SCALARS = pl.BlockSpec(memory_space=pltpu.SMEM)


def pack_body(
    lengths_ref, passages_ref, near_ref, far_ref, codes_ref, total_ref, packed_ref, sem
):
    passage_total, passage_tokens, depth = passages_ref.shape
    most = passage_tokens // CHUNK

    def place(p, at):
        length = lengths_ref[p]
        count = lax.div(length + (CHUNK - 1), CHUNK)
        last = count - 1
        packed_ref[pl.ds(at, most)] = passages_ref[p].reshape(most, CHUNK, depth)
        first_token = passages_ref[p, 0:CHUNK].astype(jnp.float32)[0:1]
        tail = passages_ref[p, pl.ds(pl.multiple_of(last * CHUNK, CHUNK), CHUNK)]
        row = lax.broadcasted_iota(jnp.int32, (CHUNK, depth), 0)
        filled = jnp.where(row < length - last * CHUNK, tail.astype(jnp.float32), first_token)
        packed_ref[pl.ds(at + last, 1)] = filled.astype(packed_ref.dtype)[None]
        codes_ref[at] = 2 * p + 1
        for k in range(1, most):
            codes_ref[at + k] = 2 * p
        return at + count

    total = lax.fori_loop(0, passage_total, place, jnp.int32(0), unroll=4)
    total_ref[0] = total
    near = near_ref.shape[0]
    copies = [
        pltpu.make_async_copy(packed_ref.at[pl.ds(0, near)], near_ref, sem.at[0]),
        pltpu.make_async_copy(packed_ref.at[pl.ds(near, far_ref.shape[0])], far_ref, sem.at[1]),
    ]
    for copy in copies:
        copy.start()

    def fill(k, carry):
        codes_ref[total + k] = 2 * passage_total + 1
        return carry

    lax.fori_loop(0, codes_ref.shape[0] - passage_total * most, fill, 0, unroll=8)
    for copy in copies:
        copy.wait()


def pack(passages, lengths):
    passage_total, passage_tokens, depth = passages.shape
    chunks = passage_total * passage_tokens // CHUNK
    near = chunks * 11 // 16 // BLOCK * BLOCK
    return pl.pallas_call(
        pack_body,
        out_shape=(
            pltpu.VMEM((near, CHUNK, depth), passages.dtype),
            pltpu.HBM((chunks - near, CHUNK, depth), passages.dtype),
            pltpu.SMEM((chunks + BLOCK,), jnp.int32),
            pltpu.SMEM((1,), jnp.int32),
        ),
        in_specs=[SCALARS, WHOLE],
        out_specs=(WHOLE, pl.BlockSpec(memory_space=pltpu.HBM), SCALARS, SCALARS),
        scratch_shapes=[
            pltpu.VMEM((chunks, CHUNK, depth), passages.dtype),
            pltpu.SemaphoreType.DMA((2,)),
        ],
        compiler_params=pltpu.CompilerParams(vmem_limit_bytes=KERNEL_VMEM),
        name="pack",
    )(lengths, passages)


def score_body(
    codes_ref,
    total_ref,
    near_ref,
    far_ref,
    queries_ref,
    scores_ref,
    turned_ref,
    best_ref,
    rows_ref,
    fetched_ref,
    sem,
):
    query_count, query_tokens, depth = queries_ref.shape
    passage_total = scores_ref.shape[1]
    columns = query_count * query_tokens
    width = min(columns, 512)
    fetch = pltpu.make_async_copy(far_ref, fetched_ref, sem)
    fetch.start()
    turned_ref[...] = queries_ref[...].reshape(columns, depth).T

    def block(i, running, packed_ref, first):
        rows = packed_ref[pl.ds((i - first) * BLOCK, BLOCK)].reshape(BLOCK * CHUNK, depth)
        after = []
        for w in range(columns // width):
            similarity = jnp.dot(
                rows,
                turned_ref[:, w * width : (w + 1) * width],
                preferred_element_type=jnp.float32,
            )
            top = running[w]
            for j in range(BLOCK):
                chunk = similarity[j * CHUNK : (j + 1) * CHUNK]
                code = codes_ref[i * BLOCK + j]
                kept = jnp.where((code & 1) == 1, NEGATIVE, top)
                top = jnp.maximum(kept, jnp.maximum(chunk[:SUBLANES], chunk[SUBLANES:]))
                at = lax.shift_right_logical(code, 1) * PITCH
                for k in range(width // LANES):
                    best_ref[w * (width // LANES) + k, pl.ds(at, SUBLANES), :] = top[
                        :, k * LANES : (k + 1) * LANES
                    ]
            after.append(top)
        return tuple(after)

    start = jnp.full((SUBLANES, width), NEGATIVE, jnp.float32)
    blocks = lax.div(total_ref[0] + (BLOCK - 1), BLOCK)
    turn = near_ref.shape[0] // BLOCK
    running = lax.fori_loop(
        0,
        jnp.minimum(blocks, turn),
        functools.partial(block, packed_ref=near_ref, first=0),
        (start,) * (columns // width),
    )
    fetch.wait()
    lax.fori_loop(
        turn, blocks, functools.partial(block, packed_ref=fetched_ref, first=turn), running
    )

    per = LANES // query_tokens
    for k in range(columns // LANES):
        for g in range(passage_total // SUBLANES):
            base = g * SUBLANES * PITCH
            top = best_ref[k, pl.ds(base, SUBLANES, stride=PITCH), :]
            for s in range(1, SUBLANES):
                top = jnp.maximum(top, best_ref[k, pl.ds(base + s, SUBLANES, stride=PITCH), :])
            rows_ref[g * SUBLANES : (g + 1) * SUBLANES, :] = top
        turned = rows_ref[...].T
        for j in range(per):
            scores_ref[k * per + j : k * per + j + 1, :] = jnp.sum(
                turned[j * query_tokens : (j + 1) * query_tokens], axis=0, keepdims=True
            )


def score_all(queries, near, far, codes, total, passage_total):
    query_total, query_tokens, depth = queries.shape
    tile = min(query_total, 32)
    columns = tile * query_tokens
    return pl.pallas_call(
        score_body,
        out_shape=jax.ShapeDtypeStruct((query_total, passage_total), jnp.float32),
        grid=(query_total // tile,),
        in_specs=[
            SCALARS,
            SCALARS,
            WHOLE,
            pl.BlockSpec(memory_space=pltpu.HBM),
            pl.BlockSpec((tile, query_tokens, depth), lambda q: (q, 0, 0)),
        ],
        out_specs=pl.BlockSpec((tile, passage_total), lambda q: (q, 0)),
        scratch_shapes=[
            pltpu.VMEM((depth, columns), jnp.bfloat16),
            pltpu.VMEM((columns // LANES, (passage_total + 1) * PITCH, LANES), jnp.float32),
            pltpu.VMEM((passage_total, LANES), jnp.float32),
            pltpu.VMEM(far.shape, far.dtype),
            pltpu.SemaphoreType.DMA,
        ],
        compiler_params=pltpu.CompilerParams(vmem_limit_bytes=KERNEL_VMEM),
        name="maxsim",
    )(codes, total, near, pltpu.with_memory_space_constraint(far, pltpu.HBM), queries)


def pick_body(table_ref, owner_ref, slot_ref, scores_ref, best_ref):
    owners, passages = table_ref.shape
    chunks = owner_ref.shape[1] // LANES

    def grid_of(ref):
        return jnp.concatenate(
            [ref[:, r * LANES : (r + 1) * LANES] for r in range(chunks)], axis=0
        )

    owner = grid_of(owner_ref)
    slot = grid_of(slot_ref)
    picked = jnp.zeros(owner.shape, jnp.float32)
    for o in range(owners):
        row = jnp.broadcast_to(table_ref[o : o + 1, :], owner.shape[:1] + (passages,))
        picked = jnp.where(owner == o, jnp.take_along_axis(row, slot, axis=1), picked)
    for r in range(chunks):
        scores_ref[:, r * LANES : (r + 1) * LANES] = picked[r : r + 1]

    square = (LANES, LANES)
    lower = lax.broadcasted_iota(jnp.int32, square, 0) < lax.broadcasted_iota(jnp.int32, square, 1)
    along = [jnp.broadcast_to(picked[r : r + 1], square) for r in range(chunks)]
    down = [a.T for a in along]
    place = lax.broadcasted_iota(jnp.int32, square, 0)
    kept = jnp.zeros(square, jnp.float32)
    for i in range(chunks):
        ahead = jnp.zeros(square, jnp.int32)
        for j in range(chunks):
            if j < i:
                wins = down[j] >= along[i]
            elif j > i:
                wins = down[j] > along[i]
            else:
                wins = (down[j] > along[i]) | ((down[j] == along[i]) & lower)
            ahead = ahead + wins.astype(jnp.int32)
        rank = jnp.sum(ahead, axis=0, keepdims=True)
        kept = kept + jnp.where(place == rank, along[i], 0.0)
    best_ref[...] = jnp.sum(kept.T, axis=0, keepdims=True)[:, : best_ref.shape[1]]


def pick(table, owner, slot):
    rows, candidates = slot.shape
    return pl.pallas_call(
        pick_body,
        out_shape=(
            jax.ShapeDtypeStruct((rows, candidates), jnp.float32),
            jax.ShapeDtypeStruct((rows, TOPK), jnp.float32),
        ),
        name="pick",
    )(table, owner, slot)


def shards(queries, passages, lengths, cand_owner, cand_slot):
    device_total = lax.axis_size("group") * lax.axis_size("shard")
    query_local, candidates = cand_slot.shape
    sent = jnp.broadcast_to(queries, (device_total,) + queries.shape[1:])
    everyone = lax.all_to_all(sent, AXES, split_axis=0, concat_axis=0, tiled=True)
    near, far, codes, total = pack(passages, lengths)
    scores = score_all(everyone, near, far, codes, total, passages.shape[0])
    table = lax.all_to_all(scores, AXES, split_axis=0, concat_axis=0, tiled=True)
    return pick(table, cand_owner.reshape(query_local, candidates), cand_slot)


def solution(mesh):
    placed = (
        P(AXES, None, None),
        P(AXES, None, None),
        P(AXES),
        P(AXES, None, None),
        P(AXES, None),
    )
    return jax.shard_map(
        shards,
        mesh=mesh,
        in_specs=placed,
        out_specs=(P(AXES, None), P(AXES, None)),
        check_vma=False,
    )
```

```python
import functools

import jax
import jax.numpy as jnp
from jax import lax
from jax.experimental import pallas as pl
from jax.experimental.pallas import tpu as pltpu
from jax.sharding import PartitionSpec as P

TOPK = 100
NEGATIVE = -1e30
LANES = 128
SUBLANES = 8
PITCH = SUBLANES + 1
CHUNK = SUBLANES
BLOCK = 128
TAIL = 32
KERNEL_VMEM = 24 << 20
AXES = ("group", "shard")
WHOLE = pl.BlockSpec(memory_space=pltpu.VMEM)
SCALARS = pl.BlockSpec(memory_space=pltpu.SMEM)


def pack_body(
    lengths_ref, passages_ref, near_ref, far_ref, codes_ref, total_ref, packed_ref, sem
):
    passage_total, passage_tokens, depth = passages_ref.shape
    most = passage_tokens // CHUNK

    def place(p, at):
        length = lengths_ref[p]
        count = lax.div(length + (CHUNK - 1), CHUNK)
        last = count - 1
        packed_ref[pl.ds(at, most)] = passages_ref[p].reshape(most, CHUNK, depth)
        first_token = passages_ref[p, 0:CHUNK].astype(jnp.float32)[0:1]
        tail = passages_ref[p, pl.ds(pl.multiple_of(last * CHUNK, CHUNK), CHUNK)]
        row = lax.broadcasted_iota(jnp.int32, (CHUNK, depth), 0)
        filled = jnp.where(row < length - last * CHUNK, tail.astype(jnp.float32), first_token)
        packed_ref[pl.ds(at + last, 1)] = filled.astype(packed_ref.dtype)[None]
        codes_ref[at] = 2 * PITCH * p + 1
        for k in range(1, most):
            codes_ref[at + k] = 2 * PITCH * p
        return at + count

    total = lax.fori_loop(0, passage_total, place, jnp.int32(0), unroll=4)
    total_ref[0] = total
    near = near_ref.shape[0]
    copies = [
        pltpu.make_async_copy(packed_ref.at[pl.ds(0, near)], near_ref, sem.at[0]),
        pltpu.make_async_copy(packed_ref.at[pl.ds(near, far_ref.shape[0])], far_ref, sem.at[1]),
    ]
    for copy in copies:
        copy.start()

    def fill(k, carry):
        codes_ref[total + k] = 2 * PITCH * passage_total + 1
        return carry

    lax.fori_loop(0, codes_ref.shape[0] - passage_total * most, fill, 0, unroll=8)
    for copy in copies:
        copy.wait()


def pack(passages, lengths):
    passage_total, passage_tokens, depth = passages.shape
    chunks = passage_total * passage_tokens // CHUNK
    near = chunks * 11 // 16 // BLOCK * BLOCK
    return pl.pallas_call(
        pack_body,
        out_shape=(
            pltpu.VMEM((near, CHUNK, depth), passages.dtype),
            pltpu.HBM((chunks - near, CHUNK, depth), passages.dtype),
            pltpu.SMEM((chunks + TAIL,), jnp.int32),
            pltpu.SMEM((1,), jnp.int32),
        ),
        in_specs=[SCALARS, WHOLE],
        out_specs=(WHOLE, pl.BlockSpec(memory_space=pltpu.HBM), SCALARS, SCALARS),
        scratch_shapes=[
            pltpu.VMEM((chunks, CHUNK, depth), passages.dtype),
            pltpu.SemaphoreType.DMA((2,)),
        ],
        compiler_params=pltpu.CompilerParams(vmem_limit_bytes=KERNEL_VMEM),
        name="pack",
    )(lengths, passages)


def score_body(
    codes_ref,
    total_ref,
    near_ref,
    far_ref,
    queries_ref,
    scores_ref,
    turned_ref,
    best_ref,
    rows_ref,
    fetched_ref,
    sem,
):
    query_count, query_tokens, depth = queries_ref.shape
    passage_total = scores_ref.shape[1]
    columns = query_count * query_tokens
    width = min(columns, 512)
    fetch = pltpu.make_async_copy(far_ref, fetched_ref, sem)
    fetch.start()
    turned_ref[...] = queries_ref[...].reshape(columns, depth).T

    def sweep(packed_ref, first, size, blocks, start, running):
        def block(i, running):
            base = start + i * size
            rows = packed_ref[pl.ds(base - first, size)].reshape(size * CHUNK, depth)
            after = []
            for w in range(columns // width):
                similarity = jnp.dot(
                    rows,
                    turned_ref[:, w * width : (w + 1) * width],
                    preferred_element_type=jnp.float32,
                )
                top = running[w]
                for j in range(size):
                    code = codes_ref[base + j]
                    kept = jnp.where((code & 1) == 1, NEGATIVE, top)
                    top = jnp.maximum(kept, similarity[j * CHUNK : (j + 1) * CHUNK])
                    at = lax.shift_right_logical(code, 1)
                    for k in range(width // LANES):
                        best_ref[w * (width // LANES) + k, pl.ds(at, SUBLANES), :] = top[
                            :, k * LANES : (k + 1) * LANES
                        ]
                after.append(top)
            return tuple(after)

        return lax.fori_loop(0, blocks, block, running)

    total = total_ref[0]
    near = near_ref.shape[0]
    full = lax.div(total, BLOCK)
    rest = lax.div(total - full * BLOCK + (TAIL - 1), TAIL)
    turn = near // BLOCK
    inside = full < turn
    running = (jnp.full((SUBLANES, width), NEGATIVE, jnp.float32),) * (columns // width)
    running = sweep(near_ref, 0, BLOCK, jnp.minimum(full, turn), 0, running)
    running = sweep(near_ref, 0, TAIL, jnp.where(inside, rest, 0), full * BLOCK, running)
    fetch.wait()
    running = sweep(fetched_ref, near, BLOCK, jnp.maximum(full - turn, 0), near, running)
    sweep(fetched_ref, near, TAIL, jnp.where(inside, 0, rest), full * BLOCK, running)

    per = LANES // query_tokens
    for k in range(columns // LANES):
        for g in range(passage_total // SUBLANES):
            base = g * SUBLANES * PITCH
            top = best_ref[k, pl.ds(base, SUBLANES, stride=PITCH), :]
            for s in range(1, SUBLANES):
                top = jnp.maximum(top, best_ref[k, pl.ds(base + s, SUBLANES, stride=PITCH), :])
            rows_ref[g * SUBLANES : (g + 1) * SUBLANES, :] = top
        turned = rows_ref[...].T
        for j in range(per):
            scores_ref[k * per + j : k * per + j + 1, :] = jnp.sum(
                turned[j * query_tokens : (j + 1) * query_tokens], axis=0, keepdims=True
            )


def score_all(queries, near, far, codes, total, passage_total):
    query_total, query_tokens, depth = queries.shape
    tile = min(query_total, 32)
    columns = tile * query_tokens
    return pl.pallas_call(
        score_body,
        out_shape=jax.ShapeDtypeStruct((query_total, passage_total), jnp.float32),
        grid=(query_total // tile,),
        in_specs=[
            SCALARS,
            SCALARS,
            WHOLE,
            pl.BlockSpec(memory_space=pltpu.HBM),
            pl.BlockSpec((tile, query_tokens, depth), lambda q: (q, 0, 0)),
        ],
        out_specs=pl.BlockSpec((tile, passage_total), lambda q: (q, 0)),
        scratch_shapes=[
            pltpu.VMEM((depth, columns), jnp.bfloat16),
            pltpu.VMEM((columns // LANES, (passage_total + 1) * PITCH, LANES), jnp.float32),
            pltpu.VMEM((passage_total, LANES), jnp.float32),
            pltpu.VMEM(far.shape, far.dtype),
            pltpu.SemaphoreType.DMA,
        ],
        compiler_params=pltpu.CompilerParams(vmem_limit_bytes=KERNEL_VMEM),
        name="maxsim",
    )(codes, total, near, pltpu.with_memory_space_constraint(far, pltpu.HBM), queries)


def pick_body(table_ref, owner_ref, slot_ref, scores_ref, best_ref):
    owners, passages = table_ref.shape
    chunks = owner_ref.shape[1] // LANES

    def grid_of(ref):
        return jnp.concatenate(
            [ref[:, r * LANES : (r + 1) * LANES] for r in range(chunks)], axis=0
        )

    owner = grid_of(owner_ref)
    slot = grid_of(slot_ref)
    picked = jnp.zeros(owner.shape, jnp.float32)
    for o in range(owners):
        row = jnp.broadcast_to(table_ref[o : o + 1, :], owner.shape[:1] + (passages,))
        picked = jnp.where(owner == o, jnp.take_along_axis(row, slot, axis=1), picked)
    for r in range(chunks):
        scores_ref[:, r * LANES : (r + 1) * LANES] = picked[r : r + 1]

    square = (LANES, LANES)
    lower = lax.broadcasted_iota(jnp.int32, square, 0) < lax.broadcasted_iota(jnp.int32, square, 1)
    along = [jnp.broadcast_to(picked[r : r + 1], square) for r in range(chunks)]
    down = [a.T for a in along]
    place = lax.broadcasted_iota(jnp.int32, square, 0)
    kept = jnp.zeros(square, jnp.float32)
    for i in range(chunks):
        ahead = jnp.zeros(square, jnp.int32)
        for j in range(chunks):
            if j < i:
                wins = down[j] >= along[i]
            elif j > i:
                wins = down[j] > along[i]
            else:
                wins = (down[j] > along[i]) | ((down[j] == along[i]) & lower)
            ahead = ahead + wins.astype(jnp.int32)
        rank = jnp.sum(ahead, axis=0, keepdims=True)
        kept = kept + jnp.where(place == rank, along[i], 0.0)
    best_ref[...] = jnp.sum(kept.T, axis=0, keepdims=True)[:, : best_ref.shape[1]]


def pick(table, owner, slot):
    rows, candidates = slot.shape
    return pl.pallas_call(
        pick_body,
        out_shape=(
            jax.ShapeDtypeStruct((rows, candidates), jnp.float32),
            jax.ShapeDtypeStruct((rows, TOPK), jnp.float32),
        ),
        in_specs=[WHOLE, WHOLE, WHOLE],
        compiler_params=pltpu.CompilerParams(vmem_limit_bytes=KERNEL_VMEM),
        name="pick",
    )(table, owner, slot)


def shards(queries, passages, lengths, cand_owner, cand_slot):
    device_total = lax.axis_size("group") * lax.axis_size("shard")
    query_local, candidates = cand_slot.shape
    sent = jnp.broadcast_to(queries, (device_total,) + queries.shape[1:])
    sent = pltpu.with_memory_space_constraint(sent, pltpu.VMEM)
    everyone = lax.all_to_all(sent, AXES, split_axis=0, concat_axis=0, tiled=True)
    near, far, codes, total = pack(passages, lengths)
    scores = score_all(everyone, near, far, codes, total, passages.shape[0])
    table = lax.all_to_all(scores, AXES, split_axis=0, concat_axis=0, tiled=True)
    table = pltpu.with_memory_space_constraint(table, pltpu.VMEM)
    return pick(table, cand_owner.reshape(query_local, candidates), cand_slot)


def solution(mesh):
    placed = (
        P(AXES, None, None),
        P(AXES, None, None),
        P(AXES),
        P(AXES, None, None),
        P(AXES, None),
    )
    return jax.shard_map(
        shards,
        mesh=mesh,
        in_specs=placed,
        out_specs=(P(AXES, None), P(AXES, None)),
        check_vma=False,
    )
```

```python
import jax
import jax.numpy as jnp
from jax import lax
from jax.experimental import pallas as pl
from jax.experimental.pallas import tpu as pltpu
from jax.sharding import PartitionSpec as P

TOPK = 100
NEGATIVE = -1e30
LANES = 128
SUBLANES = 8
PITCH = SUBLANES + 1
CHUNK = SUBLANES
BLOCK = 256
TAIL = 64
KERNEL_VMEM = 24 << 20
AXES = ("group", "shard")
WHOLE = pl.BlockSpec(memory_space=pltpu.VMEM)
SCALARS = pl.BlockSpec(memory_space=pltpu.SMEM)


def spread_body(queries_ref, sent_ref):
    half = sent_ref.shape[1]
    parts = [queries_ref[0, h * half : (h + 1) * half] for h in range(2)]

    def pair(d, carry):
        for h in range(2):
            sent_ref[2 * d + h] = parts[h]
        return carry

    lax.fori_loop(0, sent_ref.shape[0] // 2, pair, 0, unroll=8)


def spread(queries, device_total):
    _, query_tokens, depth = queries.shape
    return pl.pallas_call(
        spread_body,
        out_shape=pltpu.VMEM((device_total, query_tokens // 2, depth), queries.dtype),
        in_specs=[WHOLE],
        out_specs=WHOLE,
        compiler_params=pltpu.CompilerParams(vmem_limit_bytes=KERNEL_VMEM),
        name="spread",
    )(queries)


def pack_body(
    lengths_ref, passages_ref, near_ref, far_ref, codes_ref, total_ref, packed_ref, sem
):
    passage_total, passage_tokens, depth = passages_ref.shape
    most = passage_tokens // CHUNK

    def place(p, at):
        length = lengths_ref[p]
        count = lax.div(length + (CHUNK - 1), CHUNK)
        last = count - 1
        packed_ref[pl.ds(at, most)] = passages_ref[p].reshape(most, CHUNK, depth)
        first_token = passages_ref[p, 0:CHUNK].astype(jnp.float32)[0:1]
        tail = passages_ref[p, pl.ds(pl.multiple_of(last * CHUNK, CHUNK), CHUNK)]
        row = lax.broadcasted_iota(jnp.int32, (CHUNK, depth), 0)
        filled = jnp.where(row < length - last * CHUNK, tail.astype(jnp.float32), first_token)
        packed_ref[pl.ds(at + last, 1)] = filled.astype(packed_ref.dtype)[None]
        codes_ref[at] = 2 * PITCH * p + 1
        for k in range(1, most):
            codes_ref[at + k] = 2 * PITCH * p
        return at + count

    total = lax.fori_loop(0, passage_total, place, jnp.int32(0), unroll=4)
    total_ref[0] = total
    near = near_ref.shape[0]
    copies = [
        pltpu.make_async_copy(packed_ref.at[pl.ds(0, near)], near_ref, sem.at[0]),
        pltpu.make_async_copy(packed_ref.at[pl.ds(near, far_ref.shape[0])], far_ref, sem.at[1]),
    ]
    for copy in copies:
        copy.start()

    def fill(k, carry):
        codes_ref[total + k] = 2 * PITCH * passage_total + 1
        return carry

    lax.fori_loop(0, codes_ref.shape[0] - passage_total * most, fill, 0, unroll=8)
    for copy in copies:
        copy.wait()


def pack(passages, lengths):
    passage_total, passage_tokens, depth = passages.shape
    chunks = passage_total * passage_tokens // CHUNK
    near = chunks * 3 // 4 // BLOCK * BLOCK
    return pl.pallas_call(
        pack_body,
        out_shape=(
            pltpu.VMEM((near, CHUNK, depth), passages.dtype),
            pltpu.HBM((chunks - near, CHUNK, depth), passages.dtype),
            pltpu.SMEM((chunks + TAIL,), jnp.int32),
            pltpu.SMEM((1,), jnp.int32),
        ),
        in_specs=[SCALARS, WHOLE],
        out_specs=(WHOLE, pl.BlockSpec(memory_space=pltpu.HBM), SCALARS, SCALARS),
        scratch_shapes=[
            pltpu.VMEM((chunks, CHUNK, depth), passages.dtype),
            pltpu.SemaphoreType.DMA((2,)),
        ],
        compiler_params=pltpu.CompilerParams(vmem_limit_bytes=KERNEL_VMEM),
        name="pack",
    )(lengths, passages)


def score_body(
    codes_ref,
    total_ref,
    near_ref,
    far_ref,
    queries_ref,
    *rest_refs,
):
    *earlier_ref, scores_ref, turned_ref, best_ref, rows_ref, fetched_ref, sem = rest_refs
    query_count, query_tokens, depth = queries_ref.shape
    passage_total = scores_ref.shape[1]
    columns = query_count * query_tokens
    width = min(columns, 512)
    fetch = pltpu.make_async_copy(far_ref, fetched_ref, sem)
    fetch.start()
    turned_ref[...] = queries_ref[...].reshape(columns, depth).T

    def sweep(packed_ref, first, size, blocks, start, running):
        def block(i, running):
            base = start + i * size
            rows = packed_ref[pl.ds(base - first, size)].reshape(size * CHUNK, depth)
            after = []
            for w in range(columns // width):
                similarity = jnp.dot(
                    rows,
                    turned_ref[:, w * width : (w + 1) * width],
                    preferred_element_type=jnp.float32,
                )
                top = running[w]
                for j in range(size):
                    code = codes_ref[base + j]
                    kept = jnp.where((code & 1) == 1, NEGATIVE, top)
                    top = jnp.maximum(kept, similarity[j * CHUNK : (j + 1) * CHUNK])
                    at = lax.shift_right_logical(code, 1)
                    for k in range(width // LANES):
                        best_ref[w * (width // LANES) + k, pl.ds(at, SUBLANES), :] = top[
                            :, k * LANES : (k + 1) * LANES
                        ]
                after.append(top)
            return tuple(after)

        return lax.fori_loop(0, blocks, block, running)

    total = total_ref[0]
    near = near_ref.shape[0]
    full = lax.div(total, BLOCK)
    rest = lax.div(total - full * BLOCK + (TAIL - 1), TAIL)
    turn = near // BLOCK
    inside = full < turn
    running = (jnp.full((SUBLANES, width), NEGATIVE, jnp.float32),) * (columns // width)
    running = sweep(near_ref, 0, BLOCK, jnp.minimum(full, turn), 0, running)
    running = sweep(near_ref, 0, TAIL, jnp.where(inside, rest, 0), full * BLOCK, running)
    fetch.wait()
    running = sweep(fetched_ref, near, BLOCK, jnp.maximum(full - turn, 0), near, running)
    sweep(fetched_ref, near, TAIL, jnp.where(inside, 0, rest), full * BLOCK, running)

    per = LANES // query_tokens
    for k in range(columns // LANES):
        for g in range(passage_total // SUBLANES):
            base = g * SUBLANES * PITCH
            top = best_ref[k, pl.ds(base, SUBLANES, stride=PITCH), :]
            for s in range(1, SUBLANES):
                top = jnp.maximum(top, best_ref[k, pl.ds(base + s, SUBLANES, stride=PITCH), :])
            rows_ref[g * SUBLANES : (g + 1) * SUBLANES, :] = top
        turned = rows_ref[...].T
        for j in range(per):
            row = slice(k * per + j, k * per + j + 1)
            here = jnp.sum(
                turned[j * query_tokens : (j + 1) * query_tokens], axis=0, keepdims=True
            )
            for ref in earlier_ref:
                here = ref[row, :] + here
            scores_ref[row, :] = here


def score_all(queries, near, far, codes, total, passage_total, *earlier):
    query_total, query_tokens, depth = queries.shape
    tile = min(query_total, 32)
    columns = tile * query_tokens
    return pl.pallas_call(
        score_body,
        out_shape=jax.ShapeDtypeStruct((query_total, passage_total), jnp.float32),
        grid=(query_total // tile,),
        in_specs=[
            SCALARS,
            SCALARS,
            WHOLE,
            pl.BlockSpec(memory_space=pltpu.HBM),
            pl.BlockSpec((tile, query_tokens, depth), lambda q: (q, 0, 0)),
        ]
        + [pl.BlockSpec((tile, passage_total), lambda q: (q, 0)) for _ in earlier],
        out_specs=pl.BlockSpec((tile, passage_total), lambda q: (q, 0)),
        scratch_shapes=[
            pltpu.VMEM((depth, columns), jnp.bfloat16),
            pltpu.VMEM((columns // LANES, (passage_total + 1) * PITCH, LANES), jnp.float32),
            pltpu.VMEM((passage_total, LANES), jnp.float32),
            pltpu.VMEM(far.shape, far.dtype),
            pltpu.SemaphoreType.DMA,
        ],
        compiler_params=pltpu.CompilerParams(vmem_limit_bytes=KERNEL_VMEM),
        name="maxsim",
    )(codes, total, near, pltpu.with_memory_space_constraint(far, pltpu.HBM), queries, *earlier)


def pick_body(table_ref, owner_ref, slot_ref, scores_ref, best_ref):
    owners, passages = table_ref.shape
    chunks = owner_ref.shape[1] // LANES

    def grid_of(ref):
        return jnp.concatenate(
            [ref[:, r * LANES : (r + 1) * LANES] for r in range(chunks)], axis=0
        )

    owner = grid_of(owner_ref)
    slot = grid_of(slot_ref)
    picked = jnp.zeros(owner.shape, jnp.float32)
    for o in range(owners):
        row = jnp.broadcast_to(table_ref[o : o + 1, :], owner.shape[:1] + (passages,))
        picked = jnp.where(owner == o, jnp.take_along_axis(row, slot, axis=1), picked)
    for r in range(chunks):
        scores_ref[:, r * LANES : (r + 1) * LANES] = picked[r : r + 1]

    square = (LANES, LANES)
    lower = lax.broadcasted_iota(jnp.int32, square, 0) < lax.broadcasted_iota(jnp.int32, square, 1)
    along = [jnp.broadcast_to(picked[r : r + 1], square) for r in range(chunks)]
    down = [a.T for a in along]
    place = lax.broadcasted_iota(jnp.int32, square, 0)
    kept = jnp.zeros(square, jnp.float32)
    for i in range(chunks):
        ahead = jnp.zeros(square, jnp.int32)
        for j in range(chunks):
            if j < i:
                wins = down[j] >= along[i]
            elif j > i:
                wins = down[j] > along[i]
            else:
                wins = (down[j] > along[i]) | ((down[j] == along[i]) & lower)
            ahead = ahead + wins.astype(jnp.int32)
        rank = jnp.sum(ahead, axis=0, keepdims=True)
        kept = kept + jnp.where(place == rank, along[i], 0.0)
    best_ref[...] = jnp.sum(kept.T, axis=0, keepdims=True)[:, : best_ref.shape[1]]


def pick(table, owner, slot):
    rows, candidates = slot.shape
    return pl.pallas_call(
        pick_body,
        out_shape=(
            jax.ShapeDtypeStruct((rows, candidates), jnp.float32),
            jax.ShapeDtypeStruct((rows, TOPK), jnp.float32),
        ),
        in_specs=[WHOLE, WHOLE, WHOLE],
        compiler_params=pltpu.CompilerParams(vmem_limit_bytes=KERNEL_VMEM),
        name="pick",
    )(table, owner, slot)


def shards(queries, passages, lengths, cand_owner, cand_slot):
    device_total = lax.axis_size("group") * lax.axis_size("shard")
    query_local, candidates = cand_slot.shape
    assert query_local == 1 and device_total % 2 == 0
    halves = lax.all_to_all(
        spread(queries, device_total), AXES, split_axis=0, concat_axis=0, tiled=True
    )
    near, far, codes, total = pack(passages, lengths)
    others = lax.ppermute(halves, AXES, [(i, i ^ 1) for i in range(device_total)])
    scores = score_all(halves, near, far, codes, total, passages.shape[0])
    scores = score_all(others, near, far, codes, total, passages.shape[0], scores)
    table = lax.all_to_all(scores, AXES, split_axis=0, concat_axis=0, tiled=True)
    table = pltpu.with_memory_space_constraint(table, pltpu.VMEM)
    return pick(table, cand_owner.reshape(query_local, candidates), cand_slot)


def solution(mesh):
    placed = (
        P(AXES, None, None),
        P(AXES, None, None),
        P(AXES),
        P(AXES, None, None),
        P(AXES, None),
    )
    return jax.shard_map(
        shards,
        mesh=mesh,
        in_specs=placed,
        out_specs=(P(AXES, None), P(AXES, None)),
        check_vma=False,
    )
```
